32 devices in a mesh: grp: 2 (over x), qa: 16 (over z, y, core).
Axes of the slice: x: 2, y: 2, z: 4, core: 2. Of those that a mesh axis runs over, the one named last changes fastest.
Arguments:
- state: float32 [2, 2097152], P(None, ('grp', 'qa')), parts along dimension 1, may hold values from -6 to 6
- adjoint: float32 [2, 2097152], P(None, ('grp', 'qa')), parts along dimension 1, may hold values from -6 to 6
- gates: float32 [8, 3, 2, 128, 128], P('grp'), parts along dimension 0, may hold values from -0.375 to 0.375
Outputs:
- state_start: float32 [2, 2097152], P(None, ('grp', 'qa')), parts along dimension 1
- adjoint_start: float32 [2, 2097152], P(None, ('grp', 'qa')), parts along dimension 1
- grads: float32 [8, 3, 2, 128, 128], P('grp'), parts along dimension 0
The draws below stay inside these ranges and needn't reach their ends.
There are 2 independent parts, one for each index of `grp`. The reference program is written for one: setup_inputs(seed, part) draws one part's arguments, and reference() takes and returns one part's arrays. A program takes and returns all parts, laid end to end along the dimension named above; each array names one. Nothing has to cross between parts.
All inputs are finite; a program needn't handle non-finite values.
Results may differ from the reference program's by a relative error of at most 0.00014.
Values sent between devices are 32-bit elements; how exact they have to be, the bound alone decides.
A program may use at most 64 MiB of HBM per device.

```python
import math
import jax
import jax.numpy as jnp
from jax import lax

GATE = 128
CB = 4
ROUNDS = 4
AMPS = 1048576
N_QA = 16


def level_of(key, dims, pieces, smallest, high):
    level = 1.0
    for axis_at, blocks in pieces:
        heights = jax.random.uniform(jax.random.fold_in(jax.random.fold_in(key, 6), axis_at), (blocks,), jnp.float32, smallest / len(pieces), high / len(pieces))
        level = level * jnp.repeat(jnp.exp(heights), dims[axis_at] // blocks).reshape((-1,) + (1,) * (len(dims) - 1 - axis_at))
    return level


def bell_draw(own_key, extent, spread, reach, pieces=(), held_as=jnp.bfloat16):
    drawn = jax.random.normal(own_key, extent, jnp.float32) * spread
    if len(pieces) > 0:
        drawn = level_of(own_key, extent, pieces, -0.22, 0.18) * drawn
    return jnp.clip(drawn, min=-reach, max=reach).astype(held_as)


def setup_inputs(seed: int = 0, part: int = 0) -> dict:
    key_list = jax.random.split(jax.random.key(seed), 4)
    own_keys = jax.random.split(jax.random.fold_in(key_list[3], part), 4)
    return {
        "state": bell_draw(own_keys[0], (2, AMPS), 1.0, 6.0, ((1, 16),), jnp.float32),
        "adjoint": bell_draw(own_keys[1], (2, AMPS), 1.0, 6.0, ((1, 16),), jnp.float32),
        "gates": bell_draw(own_keys[2], (ROUNDS, 3, 2, GATE, GATE), (2 * GATE) ** -0.5, 0.375, (), jnp.float32),
    }


HIGHEST = lax.Precision.HIGHEST

def undo_left(real_gate, imag_gate, amplitudes):

    def product(matrix, values):
        return jnp.einsum('ji,pjq->piq', matrix, values, precision=HIGHEST)
    return jnp.stack([product(real_gate, amplitudes[0]) + product(imag_gate, amplitudes[1]), product(real_gate, amplitudes[1]) - product(imag_gate, amplitudes[0])])

def undo_right(real_gate, imag_gate, amplitudes):

    def product(matrix, values):
        return jnp.dot(values, matrix, precision=HIGHEST)
    return jnp.stack([product(real_gate, amplitudes[0]) + product(imag_gate, amplitudes[1]), product(real_gate, amplitudes[1]) - product(imag_gate, amplitudes[0])])

def outer_left(adjoint_part, state_part):

    def contract(first, second):
        return jnp.einsum('piq,pjq->ij', first, second, precision=HIGHEST)
    real_part = contract(adjoint_part[0], state_part[0]) + contract(adjoint_part[1], state_part[1])
    imag_part = contract(adjoint_part[1], state_part[0]) - contract(adjoint_part[0], state_part[1])
    return jnp.stack([real_part, imag_part])

def outer_right(adjoint_part, state_part):

    def contract(first, second):
        return jnp.einsum('pi,pj->ij', first, second, precision=HIGHEST)
    real_part = contract(adjoint_part[0], state_part[0]) + contract(adjoint_part[1], state_part[1])
    imag_part = contract(adjoint_part[1], state_part[0]) - contract(adjoint_part[0], state_part[1])
    return jnp.stack([real_part, imag_part])

def reference(state, adjoint, gates):
    shards = N_QA
    local_size = GATE * CB * GATE
    factor = 1.0 / math.sqrt(shards * CB * GATE)

    def exchanged(amplitudes):
        return amplitudes.reshape(2, shards, shards, local_size // shards).swapaxes(1, 2).reshape(2, shards * local_size)
    state_now = state
    adjoint_now = adjoint
    results = []
    for number in reversed(range(ROUNDS)):
        state_now = exchanged(state_now)
        adjoint_now = exchanged(adjoint_now)
        round_grads = [None, None, None]
        for position in (2, 1, 0):
            real_gate = gates[number, position, 0]
            imag_gate = gates[number, position, 1]
            if position == 1:
                layout = (2, shards * local_size // GATE, GATE)
                undoing = undo_right
                pairing = outer_right
            elif position == 0:
                layout = (2, shards, GATE, CB * GATE)
                undoing = undo_left
                pairing = outer_left
            else:
                layout = (2, shards * CB, GATE, GATE)
                undoing = undo_left
                pairing = outer_left
            before = undoing(real_gate, imag_gate, state_now.reshape(layout))
            round_grads[position] = factor * pairing(adjoint_now.reshape(layout), before)
            adjoint_now = undoing(real_gate, imag_gate, adjoint_now.reshape(layout)).reshape(2, shards * local_size)
            state_now = before.reshape(2, shards * local_size)
        results.append(jnp.stack(round_grads))
    grads = jnp.stack(results[::-1])
    return (state_now, adjoint_now, grads)
```

```python
import functools
import math

import jax
import jax.numpy as jnp
from jax import lax
from jax.experimental import pallas as pl
from jax.experimental.pallas import tpu as pltpu
from jax.sharding import PartitionSpec as P

MESH = pl.DeviceIdType.MESH
F32 = jnp.float32
BF16 = jnp.bfloat16
HIGHEST = lax.Precision.HIGHEST


def split(x):
    high = x.astype(BF16)
    return high, (x - high.astype(F32)).astype(BF16)


def dot3(left, right, dims):
    def one(a, b):
        return lax.dot_general(a, b, (dims, ((), ())), preferred_element_type=F32)

    return one(left[0], right[0]) + (one(left[0], right[1]) + one(left[1], right[0]))


def blocks_of(a, b, c, d):
    return jnp.concatenate(
        [jnp.concatenate([a, b], axis=1), jnp.concatenate([c, d], axis=1)], axis=0
    )


def right_form(real, imag):
    return tuple(blocks_of(r, -i, i, r) for r, i in zip(real, imag))


def left_form(real, imag):
    pairs = [(r.T, i.T) for r, i in zip(real, imag)]
    return tuple(blocks_of(r, i, -i, r) for r, i in pairs)


def complex_of(outer, gate):
    real = outer[:gate, :gate] + outer[gate:, gate:]
    imag = outer[gate:, :gate] - outer[:gate, gate:]
    return real, imag


def kernel(
    n, rounds, blocks, gate, factor,
    x_ref, gates_ref, out_ref, grad_ref,
    recv, sent, rows_buf, cols_buf, partial, *rest,
):
    steps = n.bit_length() - 1
    halves = rest[:steps]
    send_sem, recv_sem, own_sem, half_send, half_recv, back_send, back_recv = rest[steps:]
    me = lax.axis_index("qa")
    grp = lax.axis_index("grp")
    per = gate // n
    a2 = gate // blocks
    group = n // blocks
    piece = partial.shape[2]

    barrier = pltpu.get_barrier_semaphore()

    def greet(k, carry):
        pl.semaphore_signal(
            barrier, inc=1, device_id=(grp, lax.rem(me + k, n)), device_id_type=MESH
        )
        return carry

    lax.fori_loop(1, n, greet, 0)
    pl.semaphore_wait(barrier, n - 1)

    def source(number, which, slot):
        return sent.at[number, which, slot]

    def copy_of(number, which, k):
        there = lax.rem(me + k, n)
        return pltpu.make_async_remote_copy(
            src_ref=sent.at[number, which, there],
            dst_ref=recv.at[number, which, me],
            send_sem=send_sem.at[number, which, k],
            recv_sem=recv_sem.at[number, which, k],
            device_id=(grp, there),
            device_id_type=MESH,
        )

    def arrival_of(number, which, k):
        origin = lax.rem(me + n - k, n)
        return pltpu.make_async_remote_copy(
            src_ref=sent.at[number, which, origin],
            dst_ref=recv.at[number, which, origin],
            send_sem=send_sem.at[number, which, k],
            recv_sem=recv_sem.at[number, which, k],
            device_id=(grp, origin),
            device_id_type=MESH,
        )

    def own_of(number, which):
        return pltpu.make_async_copy(
            sent.at[number, which, me], recv.at[number, which, me], own_sem.at[number, which]
        )

    def start(number, which):
        def begin(k, carry):
            copy_of(number, which, k).start()
            return carry

        lax.fori_loop(1, n, begin, 0)
        own_of(number, which).start()

    def finish(number, which):
        def end(k, carry):
            arrival_of(number, which, k).wait_recv()
            return carry

        lax.fori_loop(1, n, end, 0)
        own_of(number, which).wait()

    def let_go(number, which):
        def end(k, carry):
            copy_of(number, which, k).wait_send()
            return carry

        lax.fori_loop(1, n, end, 0)

    for which in range(2):
        sent[0, which] = x_ref[which]
        start(0, which)

    wide = lax.broadcasted_iota(jnp.int32, (gate, gate), 0)
    tall = lax.broadcasted_iota(jnp.int32, (gate, gate), 1)
    joined = lax.rem(tall, a2) * blocks + lax.div(tall, a2)
    order = jnp.where(wide == joined, 1.0, 0.0).astype(F32)
    order_low = order.astype(BF16)

    def reordered(x):
        once = lax.dot_general(order_low, x, (((0,), (0,)), ((), ())), preferred_element_type=F32)
        return jnp.dot(once.astype(BF16), order_low, preferred_element_type=F32).astype(BF16)

    def restored(x):
        once = jnp.dot(order, x, precision=HIGHEST, preferred_element_type=F32)
        return lax.dot_general(
            once, order, (((1,), (1,)), ((), ())), precision=HIGHEST, preferred_element_type=F32
        )

    def put_grad(number, position, real, imag):
        for at, value in enumerate((real, imag)):
            first = (position * 2 + at) * gate
            value = value * factor
            low = first
            while low < first + gate:
                slot, inside = divmod(low, piece)
                high = min(first + gate, (slot + 1) * piece)
                partial[number, slot, inside : inside + high - low, :] = value[
                    low - first : high - first
                ]
                low = high

    def one_round(t, carry):
        number = rounds - 1 - t

        def gate_parts(position):
            return split(gates_ref[number, position, 0]), split(gates_ref[number, position, 1])

        real, imag = gate_parts(2)
        last = left_form([reordered(x) for x in real], [reordered(x) for x in imag])
        real, imag = gate_parts(1)
        middle = right_form(real, imag)
        real, imag = gate_parts(0)
        first = left_form(real, imag)

        inputs = []
        undone = []
        for which in range(2):
            finish(t, which)
            columns = []
            for a1 in range(blocks):
                pieces = [
                    recv[t, which, a1 * group : (a1 + 1) * group, part, c].reshape(a2, gate)
                    for part in range(2)
                    for c in range(blocks)
                ]
                columns.append(jnp.concatenate(pieces, axis=0))
            values = split(jnp.concatenate(columns, axis=1))
            result = dot3(last, values, ((1,), (0,)))
            for a1 in range(blocks):
                span = slice(a1 * gate, (a1 + 1) * gate)
                rows_buf[which, span, :gate] = result[:gate, span]
                rows_buf[which, span, gate:] = result[gate:, span]
            inputs.append(values)
            undone.append(result)
        outer = dot3(inputs[1], split(undone[0]), ((1,), (1,)))
        real, imag = complex_of(outer, gate)
        put_grad(number, 2, restored(real), restored(imag))

        inputs = []
        undone = []
        for which in range(2):
            values = split(rows_buf[which])
            result = dot3(values, middle, ((1,), (0,)))
            for a1 in range(blocks):
                for c in range(blocks):
                    low = (a1 * blocks + c) * a2
                    for part in range(2):
                        top = part * gate + a1 * a2
                        cols_buf[which, top : top + a2, c * gate : (c + 1) * gate] = result[
                            low : low + a2, part * gate : (part + 1) * gate
                        ]
            inputs.append(values)
            undone.append(result)
        outer = dot3(inputs[1], split(undone[0]), ((0,), (0,)))
        put_grad(number, 1, *complex_of(outer, gate))

        inputs = []
        undone = []
        for which in range(2):
            values = split(cols_buf[which])
            result = dot3(first, values, ((1,), (0,)))
            for part in range(2):
                for c in range(blocks):
                    block = result[
                        part * gate : (part + 1) * gate, c * gate : (c + 1) * gate
                    ].reshape(n, per, gate)
                    sent[t + 1, which, :, part, c] = block
            inputs.append(values)
            undone.append(result)

            @pl.when(t < rounds - 1)
            def _():
                start(t + 1, which)

        outer = dot3(inputs[1], split(undone[0]), ((1,), (1,)))
        put_grad(number, 0, *complex_of(outer, gate))
        return carry

    lax.fori_loop(0, rounds, one_round, 0)

    base = 0
    for s in range(steps):
        bit = 1 << s
        mine = lax.rem(lax.div(me, bit), 2)
        partner = me + (1 - 2 * mine) * bit
        size = n >> (s + 1)
        keep = base + mine * size
        give = base + (1 - mine) * size
        copy = pltpu.make_async_remote_copy(
            src_ref=partial.at[:, pl.ds(give, size)],
            dst_ref=halves[s],
            send_sem=half_send.at[s],
            recv_sem=half_recv.at[s],
            device_id=(grp, partner),
            device_id_type=MESH,
        )
        copy.start()
        if s == 0:
            for which in range(2):
                out_ref[which] = sent[rounds, which]
        copy.wait()
        if s == steps - 1:
            grad_ref[:, pl.ds(keep, size)] = partial[:, pl.ds(keep, size)] + halves[s][...]
        else:
            partial[:, pl.ds(keep, size)] = partial[:, pl.ds(keep, size)] + halves[s][...]
        base = keep
    for s in range(steps - 1, -1, -1):
        bit = 1 << s
        mine = lax.rem(lax.div(me, bit), 2)
        partner = me + (1 - 2 * mine) * bit
        size = n >> (s + 1)
        copy = pltpu.make_async_remote_copy(
            src_ref=grad_ref.at[:, pl.ds(base, size)],
            dst_ref=grad_ref.at[:, pl.ds(base, size)],
            send_sem=back_send.at[s],
            recv_sem=back_recv.at[s],
            device_id=(grp, partner),
            device_id_type=MESH,
        )
        copy.start()
        copy.wait()
        base = base - mine * size

    def release(t, carry):
        for which in range(2):
            let_go(t, which)
        return carry

    lax.fori_loop(0, rounds, release, 0)


def on_device(state, adjoint, gates):
    gate = gates.shape[-1]
    rounds = gates.shape[0]
    local_size = state.shape[1]
    n = lax.axis_size("qa")
    blocks = local_size // (gate * gate)
    per = gate // n
    factor = 1.0 / math.sqrt(n * local_size // gate)
    steps = n.bit_length() - 1
    piece = 6 * gate // n

    def inward(x):
        return x.reshape(2, n, per, blocks, gate).transpose(1, 0, 3, 2, 4)

    x = jnp.stack([inward(state), inward(adjoint)])
    amps = (2, n, 2, blocks, per, gate)
    out, grads = pl.pallas_call(
        functools.partial(kernel, n, rounds, blocks, gate, factor),
        out_shape=(
            jax.ShapeDtypeStruct(amps, F32),
            jax.ShapeDtypeStruct((rounds, n, piece, gate), F32),
        ),
        in_specs=[pl.BlockSpec(memory_space=pltpu.VMEM)] * 2,
        out_specs=(pl.BlockSpec(memory_space=pltpu.VMEM),) * 2,
        scratch_shapes=[
            pltpu.VMEM((rounds,) + amps, F32),
            pltpu.VMEM((rounds + 1,) + amps, F32),
            pltpu.VMEM((2, blocks * gate, 2 * gate), F32),
            pltpu.VMEM((2, 2 * gate, blocks * gate), F32),
            pltpu.VMEM((rounds, n, piece, gate), F32),
            *[pltpu.VMEM((rounds, n >> (s + 1), piece, gate), F32) for s in range(steps)],
            pltpu.SemaphoreType.DMA((rounds, 2, n)),
            pltpu.SemaphoreType.DMA((rounds, 2, n)),
            pltpu.SemaphoreType.DMA((rounds, 2)),
            pltpu.SemaphoreType.DMA((steps,)),
            pltpu.SemaphoreType.DMA((steps,)),
            pltpu.SemaphoreType.DMA((steps,)),
            pltpu.SemaphoreType.DMA((steps,)),
        ],
        compiler_params=pltpu.CompilerParams(
            collective_id=0, has_side_effects=True, vmem_limit_bytes=60000 * 1024
        ),
    )(x, gates)

    def outward(y):
        return y.transpose(1, 0, 3, 2, 4).reshape(2, local_size)

    return outward(out[0]), outward(out[1]), grads.reshape(gates.shape)


def solution(mesh):
    amplitudes = P(None, ("grp", "qa"))
    matrices = P("grp", None, None, None, None)
    return jax.shard_map(
        on_device,
        mesh=mesh,
        in_specs=(amplitudes, amplitudes, matrices),
        out_specs=(amplitudes, amplitudes, matrices),
        check_vma=False,
    )
```

```python
import functools
import math

import jax
import jax.numpy as jnp
from jax import lax
from jax.experimental import pallas as pl
from jax.experimental.pallas import tpu as pltpu
from jax.sharding import PartitionSpec as P

MESH = pl.DeviceIdType.MESH
F32 = jnp.float32
BF16 = jnp.bfloat16
HIGHEST = lax.Precision.HIGHEST


def split(x):
    high = x.astype(BF16)
    return high, (x - high.astype(F32)).astype(BF16)


def dot3(left, right, dims):
    def one(a, b):
        return lax.dot_general(a, b, (dims, ((), ())), preferred_element_type=F32)

    return one(left[0], right[0]) + (one(left[0], right[1]) + one(left[1], right[0]))


def blocks_of(a, b, c, d):
    return jnp.concatenate(
        [jnp.concatenate([a, b], axis=1), jnp.concatenate([c, d], axis=1)], axis=0
    )


def right_form(real, imag):
    return tuple(blocks_of(r, -i, i, r) for r, i in zip(real, imag))


def left_form(real, imag):
    pairs = [(r.T, i.T) for r, i in zip(real, imag)]
    return tuple(blocks_of(r, i, -i, r) for r, i in pairs)


def complex_of(outer, gate):
    real = outer[:gate, :gate] + outer[gate:, gate:]
    imag = outer[gate:, :gate] - outer[:gate, gate:]
    return real, imag


def kernel(
    n, rounds, blocks, gate, factor,
    x_ref, gates_ref, out_ref, grad_ref,
    recv, sent, rows_buf, cols_buf, wide_before, tall_before, partial, *rest,
):
    steps = n.bit_length() - 1
    halves = rest[:steps]
    send_sem, recv_sem, own_sem, sum_send, sum_recv = rest[steps:]
    me = lax.axis_index("qa")
    grp = lax.axis_index("grp")
    per = gate // n
    a2 = gate // blocks
    group = n // blocks
    piece = partial.shape[2]

    barrier = pltpu.get_barrier_semaphore()

    def greet(k, carry):
        pl.semaphore_signal(
            barrier, inc=1, device_id=(grp, lax.rem(me + k, n)), device_id_type=MESH
        )
        return carry

    lax.fori_loop(1, n, greet, 0)
    pl.semaphore_wait(barrier, n - 1)

    def copy_of(number, which, k):
        there = lax.rem(me + k, n)
        return pltpu.make_async_remote_copy(
            src_ref=sent.at[number, which, there],
            dst_ref=recv.at[number, which, me],
            send_sem=send_sem.at[number, which, k],
            recv_sem=recv_sem.at[number, which, k],
            device_id=(grp, there),
            device_id_type=MESH,
        )

    def arrival_of(number, which, k):
        origin = lax.rem(me + n - k, n)
        return pltpu.make_async_remote_copy(
            src_ref=sent.at[number, which, origin],
            dst_ref=recv.at[number, which, origin],
            send_sem=send_sem.at[number, which, k],
            recv_sem=recv_sem.at[number, which, k],
            device_id=(grp, origin),
            device_id_type=MESH,
        )

    def own_of(number, which):
        return pltpu.make_async_copy(
            sent.at[number, which, me], recv.at[number, which, me], own_sem.at[number, which]
        )

    def start(number, which):
        def begin(k, carry):
            copy_of(number, which, k).start()
            return carry

        lax.fori_loop(1, n, begin, 0)
        own_of(number, which).start()

    def finish(number, which):
        def end(k, carry):
            arrival_of(number, which, k).wait_recv()
            return carry

        lax.fori_loop(1, n, end, 0)
        own_of(number, which).wait()

    def let_go(number, which):
        def end(k, carry):
            copy_of(number, which, k).wait_send()
            return carry

        lax.fori_loop(1, n, end, 0)

    stages = 2 * steps
    bits = [lax.rem(lax.div(me, 1 << s), 2) for s in range(steps)]
    bases = [0]
    for s in range(steps):
        bases.append(bases[-1] + bits[s] * (n >> (s + 1)))

    def sum_copy(t, stage):
        number = rounds - 1 - t
        s = stage if stage < steps else stages - 1 - stage
        size = n >> (s + 1)
        if stage < steps:
            give = bases[s] + (1 - bits[s]) * size
            source = partial.at[number, pl.ds(give, size)]
            target = halves[s].at[number]
        else:
            source = grad_ref.at[number, pl.ds(bases[s + 1], size)]
            target = source
        return pltpu.make_async_remote_copy(
            src_ref=source,
            dst_ref=target,
            send_sem=sum_send.at[number, stage],
            recv_sem=sum_recv.at[number, stage],
            device_id=(grp, me + (1 - 2 * bits[s]) * (1 << s)),
            device_id_type=MESH,
        )

    def sum_end(t, stage):
        number = rounds - 1 - t
        sum_copy(t, stage).wait()
        if stage < steps:
            size = n >> (stage + 1)
            keep = pl.ds(bases[stage + 1], size)
            total = partial[number, keep] + halves[stage][number]
            if stage == steps - 1:
                grad_ref[number, keep] = total
            else:
                partial[number, keep] = total

    def tick(t, at):
        for lag in range(1, rounds):
            stage = 2 * lag - 1 + at
            if stage < stages:

                @pl.when(t >= lag)
                def _(lag=lag, stage=stage):
                    sum_end(t - lag, stage - 1)
                    sum_copy(t - lag, stage).start()

    for which in range(2):
        sent[0, which] = x_ref[which]
        start(0, which)

    wide = lax.broadcasted_iota(jnp.int32, (gate, gate), 0)
    tall = lax.broadcasted_iota(jnp.int32, (gate, gate), 1)
    joined = lax.rem(tall, a2) * blocks + lax.div(tall, a2)
    order = jnp.where(wide == joined, 1.0, 0.0).astype(F32)
    order_low = order.astype(BF16)

    def reordered(x):
        once = lax.dot_general(order_low, x, (((0,), (0,)), ((), ())), preferred_element_type=F32)
        return jnp.dot(once.astype(BF16), order_low, preferred_element_type=F32).astype(BF16)

    def restored(x):
        once = jnp.dot(order, x, precision=HIGHEST, preferred_element_type=F32)
        return lax.dot_general(
            once, order, (((1,), (1,)), ((), ())), precision=HIGHEST, preferred_element_type=F32
        )

    def put_grad(number, position, real, imag):
        for at, value in enumerate((real, imag)):
            first = (position * 2 + at) * gate
            value = value * factor
            low = first
            while low < first + gate:
                slot, inside = divmod(low, piece)
                high = min(first + gate, (slot + 1) * piece)
                partial[number, slot, inside : inside + high - low, :] = value[
                    low - first : high - first
                ]
                low = high

    def keep(ref, at, pair):
        for i in range(2):
            ref[at, i] = pair[i]

    def kept(ref, at):
        return ref[at, 0], ref[at, 1]

    def one_round(t, carry):
        number = rounds - 1 - t

        def gate_parts(position):
            return split(gates_ref[number, position, 0]), split(gates_ref[number, position, 1])

        real, imag = gate_parts(2)
        last = left_form([reordered(x) for x in real], [reordered(x) for x in imag])
        real, imag = gate_parts(1)
        middle = right_form(real, imag)
        real, imag = gate_parts(0)
        first = left_form(real, imag)

        for which in range(2):
            finish(t, which)
            tick(t, which)

            columns = []
            for a1 in range(blocks):
                pieces = [
                    recv[t, which, a1 * group : (a1 + 1) * group, part, c].reshape(a2, gate)
                    for part in range(2)
                    for c in range(blocks)
                ]
                columns.append(jnp.concatenate(pieces, axis=0))
            values = split(jnp.concatenate(columns, axis=1))
            result = dot3(last, values, ((1,), (0,)))
            for a1 in range(blocks):
                span = slice(a1 * gate, (a1 + 1) * gate)
                rows_buf[span, :gate] = result[:gate, span]
                rows_buf[span, gate:] = result[gate:, span]
            if which == 0:
                keep(wide_before, 0, split(result))
            else:
                outer = dot3(values, kept(wide_before, 0), ((1,), (1,)))
                real, imag = complex_of(outer, gate)
                put_grad(number, 2, restored(real), restored(imag))

            values = split(rows_buf[...])
            result = dot3(values, middle, ((1,), (0,)))
            for a1 in range(blocks):
                for c in range(blocks):
                    low = (a1 * blocks + c) * a2
                    for part in range(2):
                        top = part * gate + a1 * a2
                        cols_buf[top : top + a2, c * gate : (c + 1) * gate] = result[
                            low : low + a2, part * gate : (part + 1) * gate
                        ]
            if which == 0:
                keep(tall_before, 0, split(result))
            else:
                outer = dot3(values, kept(tall_before, 0), ((0,), (0,)))
                put_grad(number, 1, *complex_of(outer, gate))

            values = split(cols_buf[...])
            result = dot3(first, values, ((1,), (0,)))
            for part in range(2):
                for c in range(blocks):
                    block = result[
                        part * gate : (part + 1) * gate, c * gate : (c + 1) * gate
                    ].reshape(n, per, gate)
                    sent[t + 1, which, :, part, c] = block

            @pl.when(t < rounds - 1)
            def _():
                start(t + 1, which)

            if which == 0:
                keep(wide_before, 1, split(result))
            else:
                outer = dot3(values, kept(wide_before, 1), ((1,), (1,)))
                put_grad(number, 0, *complex_of(outer, gate))
        sum_copy(t, 0).start()
        return carry

    lax.fori_loop(0, rounds, one_round, 0)

    for which in range(2):
        out_ref[which] = sent[rounds, which]
    for stage in range(stages):
        now = [t for t in range(rounds) if min(2 * (rounds - 1 - t), stages - 1) <= stage]
        for t in now:
            sum_end(t, stage)
            if stage + 1 < stages:
                sum_copy(t, stage + 1).start()

    def release(t, carry):
        for which in range(2):
            let_go(t, which)
        return carry

    lax.fori_loop(0, rounds, release, 0)


def on_device(state, adjoint, gates):
    gate = gates.shape[-1]
    rounds = gates.shape[0]
    local_size = state.shape[1]
    n = lax.axis_size("qa")
    blocks = local_size // (gate * gate)
    per = gate // n
    factor = 1.0 / math.sqrt(n * local_size // gate)
    steps = n.bit_length() - 1
    piece = 6 * gate // n

    def inward(x):
        return x.reshape(2, n, per, blocks, gate).transpose(1, 0, 3, 2, 4)

    x = jnp.stack([inward(state), inward(adjoint)])
    amps = (2, n, 2, blocks, per, gate)
    out, grads = pl.pallas_call(
        functools.partial(kernel, n, rounds, blocks, gate, factor),
        out_shape=(
            jax.ShapeDtypeStruct(amps, F32),
            jax.ShapeDtypeStruct((rounds, n, piece, gate), F32),
        ),
        in_specs=[pl.BlockSpec(memory_space=pltpu.VMEM)] * 2,
        out_specs=(pl.BlockSpec(memory_space=pltpu.VMEM),) * 2,
        scratch_shapes=[
            pltpu.VMEM((rounds,) + amps, F32),
            pltpu.VMEM((rounds + 1,) + amps, F32),
            pltpu.VMEM((blocks * gate, 2 * gate), F32),
            pltpu.VMEM((2 * gate, blocks * gate), F32),
            pltpu.VMEM((2, 2, 2 * gate, blocks * gate), BF16),
            pltpu.VMEM((1, 2, blocks * gate, 2 * gate), BF16),
            pltpu.VMEM((rounds, n, piece, gate), F32),
            *[pltpu.VMEM((rounds, n >> (s + 1), piece, gate), F32) for s in range(steps)],
            pltpu.SemaphoreType.DMA((rounds, 2, n)),
            pltpu.SemaphoreType.DMA((rounds, 2, n)),
            pltpu.SemaphoreType.DMA((rounds, 2)),
            pltpu.SemaphoreType.DMA((rounds, 2 * steps)),
            pltpu.SemaphoreType.DMA((rounds, 2 * steps)),
        ],
        compiler_params=pltpu.CompilerParams(
            collective_id=0, has_side_effects=True, vmem_limit_bytes=60000 * 1024
        ),
    )(x, gates)

    def outward(y):
        return y.transpose(1, 0, 3, 2, 4).reshape(2, local_size)

    return outward(out[0]), outward(out[1]), grads.reshape(gates.shape)


def solution(mesh):
    amplitudes = P(None, ("grp", "qa"))
    matrices = P("grp", None, None, None, None)
    return jax.shard_map(
        on_device,
        mesh=mesh,
        in_specs=(amplitudes, amplitudes, matrices),
        out_specs=(amplitudes, amplitudes, matrices),
        check_vma=False,
    )
```

```python
import functools
import math

import jax
import jax.numpy as jnp
from jax import lax
from jax.experimental import pallas as pl
from jax.experimental.pallas import tpu as pltpu
from jax.sharding import PartitionSpec as P

MESH = pl.DeviceIdType.MESH
F32 = jnp.float32
BF16 = jnp.bfloat16
HIGHEST = lax.Precision.HIGHEST


def split(x):
    high = x.astype(BF16)
    return high, (x - high.astype(F32)).astype(BF16)


def dot3(left, right, dims):
    def one(a, b):
        return lax.dot_general(a, b, (dims, ((), ())), preferred_element_type=F32)

    return one(left[0], right[0]) + (one(left[0], right[1]) + one(left[1], right[0]))


def blocks_of(a, b, c, d):
    return jnp.concatenate(
        [jnp.concatenate([a, b], axis=1), jnp.concatenate([c, d], axis=1)], axis=0
    )


def right_form(real, imag):
    return tuple(blocks_of(r, -i, i, r) for r, i in zip(real, imag))


def left_form(real, imag):
    pairs = [(r.T, i.T) for r, i in zip(real, imag)]
    return tuple(blocks_of(r, i, -i, r) for r, i in pairs)


def complex_of(outer, gate):
    real = outer[:gate, :gate] + outer[gate:, gate:]
    imag = outer[gate:, :gate] - outer[:gate, gate:]
    return real, imag


def kernel(
    n, rounds, blocks, gate, factor,
    state_ref, adjoint_ref, gates_ref, state_out, adjoint_out, grad_ref,
    recv, sent, rows_buf, cols_buf, wide_before, tall_before, partial, *rest,
):
    steps = n.bit_length() - 1
    halves = rest[:steps]
    send_sem, recv_sem, own_sem, sum_send, sum_recv = rest[steps:]
    me = lax.axis_index("qa")
    grp = lax.axis_index("grp")
    per = gate // n
    a2 = gate // blocks
    group = n // blocks
    piece = partial.shape[3]

    barrier = pltpu.get_barrier_semaphore()

    def greet(k, carry):
        pl.semaphore_signal(
            barrier, inc=1, device_id=(grp, lax.rem(me + k, n)), device_id_type=MESH
        )
        return carry

    lax.fori_loop(1, n, greet, 0)
    pl.semaphore_wait(barrier, n - 1)

    def copy_of(number, which, k):
        there = lax.rem(me + k, n)
        return pltpu.make_async_remote_copy(
            src_ref=sent.at[number, which, there],
            dst_ref=recv.at[number, which, me],
            send_sem=send_sem.at[number, which, k],
            recv_sem=recv_sem.at[number, which, k],
            device_id=(grp, there),
            device_id_type=MESH,
        )

    def arrival_of(number, which, k):
        origin = lax.rem(me + n - k, n)
        return pltpu.make_async_remote_copy(
            src_ref=sent.at[number, which, origin],
            dst_ref=recv.at[number, which, origin],
            send_sem=send_sem.at[number, which, k],
            recv_sem=recv_sem.at[number, which, k],
            device_id=(grp, origin),
            device_id_type=MESH,
        )

    def own_of(number, which):
        return pltpu.make_async_copy(
            sent.at[number, which, me], recv.at[number, which, me], own_sem.at[number, which]
        )

    def start(number, which):
        def begin(k, carry):
            copy_of(number, which, k).start()
            return carry

        lax.fori_loop(1, n, begin, 0)
        own_of(number, which).start()

    def finish(number, which):
        def end(k, carry):
            arrival_of(number, which, k).wait_recv()
            return carry

        lax.fori_loop(1, n, end, 0)
        own_of(number, which).wait()

    def let_go(number, which):
        def end(k, carry):
            copy_of(number, which, k).wait_send()
            return carry

        lax.fori_loop(1, n, end, 0)

    stages = 2 * steps
    bits = [lax.rem(lax.div(me, 1 << s), 2) for s in range(steps)]
    bases = [0]
    for s in range(steps):
        bases.append(bases[-1] + bits[s] * (n >> (s + 1)))

    def part_of(ref, number, low, size, position):
        if position is None:
            return ref.at[number, pl.ds(low, size)]
        return ref.at[number, pl.ds(low, size), position]

    def sum_copy(t, position, stage):
        number = rounds - 1 - t
        s = stage if stage < steps else stages - 1 - stage
        size = n >> (s + 1)
        if stage < steps:
            give = bases[s] + (1 - bits[s]) * size
            source = part_of(partial, number, give, size, position)
            target = part_of(halves[s], number, 0, size, position)
        else:
            source = part_of(grad_ref, number, bases[s + 1], size, position)
            target = source
        own = 0 if position is None else position
        return pltpu.make_async_remote_copy(
            src_ref=source,
            dst_ref=target,
            send_sem=sum_send.at[number, stage, own],
            recv_sem=sum_recv.at[number, stage, own],
            device_id=(grp, me + (1 - 2 * bits[s]) * (1 << s)),
            device_id_type=MESH,
        )

    def sum_end(t, position, stage):
        number = rounds - 1 - t
        sum_copy(t, position, stage).wait()
        if stage < steps:
            size = n >> (stage + 1)
            base = bases[stage + 1]
            mine = part_of(partial, number, base, size, position)
            total = mine[...] + part_of(halves[stage], number, 0, size, position)[...]
            if stage == steps - 1:
                part_of(grad_ref, number, base, size, position)[...] = total
            else:
                mine[...] = total

    def advance(t, position, stage):
        sum_end(t, position, stage)
        if stage + 1 < stages:
            sum_copy(t, position, stage + 1).start()

    def tick(t, at):
        for lag in range(1, rounds):
            stage = 4 * (lag - 1) + at
            if stage < stages:

                @pl.when(t >= lag)
                def _(lag=lag, stage=stage):
                    advance(t - lag, None, stage)

    stride = 2 * blocks
    for which, ref in enumerate((state_ref, adjoint_ref)):
        for part in range(2):
            for c in range(blocks):
                rows = ref[pl.ds(2 * c + part, gate, stride=stride), :]
                sent[0, which, :, part, c] = rows.reshape(n, per, gate)
        start(0, which)

    wide = lax.broadcasted_iota(jnp.int32, (gate, gate), 0)
    tall = lax.broadcasted_iota(jnp.int32, (gate, gate), 1)
    joined = lax.rem(tall, a2) * blocks + lax.div(tall, a2)
    order = jnp.where(wide == joined, 1.0, 0.0).astype(F32)
    order_low = order.astype(BF16)

    def reordered(x):
        once = lax.dot_general(order_low, x, (((0,), (0,)), ((), ())), preferred_element_type=F32)
        return jnp.dot(once.astype(BF16), order_low, preferred_element_type=F32).astype(BF16)

    def restored(x):
        once = jnp.dot(order, x, precision=HIGHEST, preferred_element_type=F32)
        return lax.dot_general(
            once, order, (((1,), (1,)), ((), ())), precision=HIGHEST, preferred_element_type=F32
        )

    def put_grad(t, position, real, imag):
        value = jnp.concatenate([real, imag], axis=0) * factor
        partial[rounds - 1 - t, :, position] = value.reshape(n, piece, gate)

        @pl.when(t == rounds - 1)
        def _():
            for earlier in range(2, position, -1):
                advance(t, earlier, earlier - position - 1)
            sum_copy(t, position, 0).start()

    def keep(ref, at, pair):
        for i in range(2):
            ref[at, i] = pair[i]

    def kept(ref, at):
        return ref[at, 0], ref[at, 1]

    def one_round(t, carry):
        number = rounds - 1 - t

        def gate_parts(position):
            return split(gates_ref[number, position, 0]), split(gates_ref[number, position, 1])

        real, imag = gate_parts(2)
        last = left_form([reordered(x) for x in real], [reordered(x) for x in imag])
        real, imag = gate_parts(1)
        middle = right_form(real, imag)
        real, imag = gate_parts(0)
        first = left_form(real, imag)

        for which in range(2):
            finish(t, which)
            tick(t, 2 * which)

            columns = []
            for a1 in range(blocks):
                pieces = [
                    recv[t, which, a1 * group : (a1 + 1) * group, part, c].reshape(a2, gate)
                    for part in range(2)
                    for c in range(blocks)
                ]
                columns.append(jnp.concatenate(pieces, axis=0))
            values = split(jnp.concatenate(columns, axis=1))
            result = dot3(last, values, ((1,), (0,)))
            for a1 in range(blocks):
                span = slice(a1 * gate, (a1 + 1) * gate)
                rows_buf[span, :gate] = result[:gate, span]
                rows_buf[span, gate:] = result[gate:, span]
            if which == 0:
                keep(wide_before, 0, split(result))
            else:
                outer = dot3(values, kept(wide_before, 0), ((1,), (1,)))
                real, imag = complex_of(outer, gate)
                put_grad(t, 2, restored(real), restored(imag))

            values = split(rows_buf[...])
            result = dot3(values, middle, ((1,), (0,)))
            for a1 in range(blocks):
                for c in range(blocks):
                    low = (a1 * blocks + c) * a2
                    for part in range(2):
                        top = part * gate + a1 * a2
                        cols_buf[top : top + a2, c * gate : (c + 1) * gate] = result[
                            low : low + a2, part * gate : (part + 1) * gate
                        ]
            if which == 0:
                keep(tall_before, 0, split(result))
            else:
                outer = dot3(values, kept(tall_before, 0), ((0,), (0,)))
                put_grad(t, 1, *complex_of(outer, gate))

            values = split(cols_buf[...])
            result = dot3(first, values, ((1,), (0,)))
            for part in range(2):
                for c in range(blocks):
                    block = result[
                        part * gate : (part + 1) * gate, c * gate : (c + 1) * gate
                    ].reshape(n, per, gate)
                    sent[t + 1, which, :, part, c] = block

            @pl.when(t < rounds - 1)
            def _():
                start(t + 1, which)

            if which == 0:
                keep(wide_before, 1, split(result))
                tick(t, 1)
            else:
                outer = dot3(values, kept(wide_before, 1), ((1,), (1,)))
                put_grad(t, 0, *complex_of(outer, gate))
        tick(t, 3)

        @pl.when(t < rounds - 1)
        def _():
            sum_copy(t, None, 0).start()

        return carry

    lax.fori_loop(0, rounds, one_round, 0)

    for which, ref in enumerate((state_out, adjoint_out)):
        for part in range(2):
            for c in range(blocks):
                rows = sent[rounds, which, :, part, c].reshape(gate, gate)
                ref[pl.ds(2 * c + part, gate, stride=stride), :] = rows
    units = [(t, None, 4 * (rounds - 1 - t)) for t in range(rounds - 1)]
    units += [(rounds - 1, position, position) for position in (2, 1, 0)]
    units = [unit for unit in units if unit[2] < stages]
    while units:
        for unit in units:
            advance(*unit)
        units = [(t, position, stage + 1) for t, position, stage in units if stage + 1 < stages]

    def release(t, carry):
        for which in range(2):
            let_go(t, which)
        return carry

    lax.fori_loop(0, rounds, release, 0)


def on_device(state, adjoint, gates):
    gate = gates.shape[-1]
    rounds = gates.shape[0]
    local_size = state.shape[1]
    n = lax.axis_size("qa")
    blocks = local_size // (gate * gate)
    per = gate // n
    factor = 1.0 / math.sqrt(n * local_size // gate)
    steps = n.bit_length() - 1
    piece = 2 * gate // n
    amps = (2, n, 2, blocks, per, gate)
    flat = (2 * local_size // gate, gate)
    sums = (rounds, n, 3, piece, gate)

    def inward(x):
        return x.reshape(2, local_size // gate, gate).swapaxes(0, 1).reshape(flat)

    state_out, adjoint_out, grads = pl.pallas_call(
        functools.partial(kernel, n, rounds, blocks, gate, factor),
        out_shape=(
            jax.ShapeDtypeStruct(flat, F32),
            jax.ShapeDtypeStruct(flat, F32),
            jax.ShapeDtypeStruct(sums, F32),
        ),
        in_specs=[pl.BlockSpec(memory_space=pltpu.VMEM)] * 3,
        out_specs=(pl.BlockSpec(memory_space=pltpu.VMEM),) * 3,
        scratch_shapes=[
            pltpu.VMEM((rounds,) + amps, F32),
            pltpu.VMEM((rounds + 1,) + amps, F32),
            pltpu.VMEM((blocks * gate, 2 * gate), F32),
            pltpu.VMEM((2 * gate, blocks * gate), F32),
            pltpu.VMEM((2, 2, 2 * gate, blocks * gate), BF16),
            pltpu.VMEM((1, 2, blocks * gate, 2 * gate), BF16),
            pltpu.VMEM(sums, F32),
            *[pltpu.VMEM((rounds, n >> (s + 1)) + sums[2:], F32) for s in range(steps)],
            pltpu.SemaphoreType.DMA((rounds, 2, n)),
            pltpu.SemaphoreType.DMA((rounds, 2, n)),
            pltpu.SemaphoreType.DMA((rounds, 2)),
            pltpu.SemaphoreType.DMA((rounds, 2 * steps, 3)),
            pltpu.SemaphoreType.DMA((rounds, 2 * steps, 3)),
        ],
        compiler_params=pltpu.CompilerParams(
            collective_id=0, has_side_effects=True, vmem_limit_bytes=60000 * 1024
        ),
    )(inward(state), inward(adjoint), gates)

    def outward(y):
        return y.reshape(local_size // gate, 2, gate).swapaxes(0, 1).reshape(2, local_size)

    return outward(state_out), outward(adjoint_out), grads.swapaxes(1, 2).reshape(gates.shape)


def solution(mesh):
    amplitudes = P(None, ("grp", "qa"))
    matrices = P("grp", None, None, None, None)
    return jax.shard_map(
        on_device,
        mesh=mesh,
        in_specs=(amplitudes, amplitudes, matrices),
        out_specs=(amplitudes, amplitudes, matrices),
        check_vma=False,
    )
```

```python
import functools
import math

import jax
import jax.numpy as jnp
from jax import lax
from jax.experimental import pallas as pl
from jax.experimental.pallas import tpu as pltpu
from jax.sharding import PartitionSpec as P

MESH = pl.DeviceIdType.MESH
F32 = jnp.float32
BF16 = jnp.bfloat16
HIGHEST = lax.Precision.HIGHEST


def split(x):
    high = x.astype(BF16)
    return high, (x - high.astype(F32)).astype(BF16)


def dot3(left, right, dims):
    def one(a, b):
        return lax.dot_general(a, b, (dims, ((), ())), preferred_element_type=F32)

    return one(left[0], right[0]) + (one(left[0], right[1]) + one(left[1], right[0]))


def blocks_of(a, b, c, d):
    return jnp.concatenate(
        [jnp.concatenate([a, b], axis=1), jnp.concatenate([c, d], axis=1)], axis=0
    )


def right_form(real, imag):
    return tuple(blocks_of(r, -i, i, r) for r, i in zip(real, imag))


def left_form(real, imag):
    pairs = [(r.T, i.T) for r, i in zip(real, imag)]
    return tuple(blocks_of(r, i, -i, r) for r, i in pairs)


def complex_of(outer, gate):
    real = outer[:gate, :gate] + outer[gate:, gate:]
    imag = outer[gate:, :gate] - outer[:gate, gate:]
    return real, imag


def kernel(
    n, rounds, blocks, gate, factor,
    state_ref, adjoint_ref, gates_ref, state_out, adjoint_out, grad_ref,
    recv, sent, rows_buf, cols_buf, wide_before, tall_before, partial, *rest,
):
    steps = n.bit_length() - 1
    halves = rest[:steps]
    send_sem, recv_sem, own_sem, sum_send, sum_recv = rest[steps:]
    me = lax.axis_index("qa")
    grp = lax.axis_index("grp")
    per = gate // n
    a2 = gate // blocks
    group = n // blocks
    piece = partial.shape[3]

    barrier = pltpu.get_barrier_semaphore()

    def greet(k, carry):
        pl.semaphore_signal(
            barrier, inc=1, device_id=(grp, lax.rem(me + k, n)), device_id_type=MESH
        )
        return carry

    lax.fori_loop(1, n, greet, 0)
    pl.semaphore_wait(barrier, n - 1)

    def copy_of(number, which, k):
        there = lax.rem(me + k, n)
        return pltpu.make_async_remote_copy(
            src_ref=sent.at[number, which, there],
            dst_ref=recv.at[number, which, me],
            send_sem=send_sem.at[number, which, k],
            recv_sem=recv_sem.at[number, which, k],
            device_id=(grp, there),
            device_id_type=MESH,
        )

    def arrival_of(number, which, k):
        origin = lax.rem(me + n - k, n)
        return pltpu.make_async_remote_copy(
            src_ref=sent.at[number, which, origin],
            dst_ref=recv.at[number, which, origin],
            send_sem=send_sem.at[number, which, k],
            recv_sem=recv_sem.at[number, which, k],
            device_id=(grp, origin),
            device_id_type=MESH,
        )

    def own_of(number, which):
        return pltpu.make_async_copy(
            sent.at[number, which, me], recv.at[number, which, me], own_sem.at[number, which]
        )

    def start(number, which):
        def begin(i, carry):
            k = n // 2 + lax.div(i + 1, 2) * (1 - 2 * lax.rem(i, 2))
            copy_of(number, which, k).start()
            return carry

        lax.fori_loop(0, n - 1, begin, 0)
        own_of(number, which).start()

    def finish(number, which):
        def end(k, carry):
            arrival_of(number, which, k).wait_recv()
            return carry

        lax.fori_loop(1, n, end, 0)
        own_of(number, which).wait()

    def let_go(number, which):
        def end(k, carry):
            copy_of(number, which, k).wait_send()
            return carry

        lax.fori_loop(1, n, end, 0)

    stages = 2 * steps
    bits = [lax.rem(lax.div(me, 1 << s), 2) for s in range(steps)]
    bases = [0]
    for s in range(steps):
        bases.append(bases[-1] + bits[s] * (n >> (s + 1)))

    def part_of(ref, number, low, size, position):
        if position is None:
            return ref.at[number, pl.ds(low, size)]
        return ref.at[number, pl.ds(low, size), position]

    def sum_copy(t, position, stage):
        number = rounds - 1 - t
        s = stage if stage < steps else stages - 1 - stage
        size = n >> (s + 1)
        if stage < steps:
            give = bases[s] + (1 - bits[s]) * size
            source = part_of(partial, number, give, size, position)
            target = part_of(halves[s], number, 0, size, position)
        else:
            source = part_of(grad_ref, number, bases[s + 1], size, position)
            target = source
        own = 0 if position is None else position
        return pltpu.make_async_remote_copy(
            src_ref=source,
            dst_ref=target,
            send_sem=sum_send.at[number, stage, own],
            recv_sem=sum_recv.at[number, stage, own],
            device_id=(grp, me + (1 - 2 * bits[s]) * (1 << s)),
            device_id_type=MESH,
        )

    def sum_end(t, position, stage):
        number = rounds - 1 - t
        sum_copy(t, position, stage).wait()
        if stage < steps:
            size = n >> (stage + 1)
            base = bases[stage + 1]
            mine = part_of(partial, number, base, size, position)
            total = mine[...] + part_of(halves[stage], number, 0, size, position)[...]
            if stage == steps - 1:
                part_of(grad_ref, number, base, size, position)[...] = total
            else:
                mine[...] = total

    def advance(t, position, stage):
        sum_end(t, position, stage)
        if stage + 1 < stages:
            sum_copy(t, position, stage + 1).start()

    def tick(t, at):
        for lag in range(1, rounds):
            stage = 2 * (lag - 1) + at
            if stage < stages:

                @pl.when(t >= lag)
                def _(lag=lag, stage=stage):
                    advance(t - lag, None, stage)

    stride = 2 * blocks
    for which, ref in enumerate((state_ref, adjoint_ref)):
        for part in range(2):
            for c in range(blocks):
                rows = ref[pl.ds(2 * c + part, gate, stride=stride), :]
                sent[0, which, :, part, c] = rows.reshape(n, per, gate)
        start(0, which)

    wide = lax.broadcasted_iota(jnp.int32, (gate, gate), 0)
    tall = lax.broadcasted_iota(jnp.int32, (gate, gate), 1)
    joined = lax.rem(tall, a2) * blocks + lax.div(tall, a2)
    order = jnp.where(wide == joined, 1.0, 0.0).astype(F32)
    order_low = order.astype(BF16)

    def reordered(x):
        once = lax.dot_general(order_low, x, (((0,), (0,)), ((), ())), preferred_element_type=F32)
        return jnp.dot(once.astype(BF16), order_low, preferred_element_type=F32).astype(BF16)

    def restored(x):
        once = jnp.dot(order, x, precision=HIGHEST, preferred_element_type=F32)
        return lax.dot_general(
            once, order, (((1,), (1,)), ((), ())), precision=HIGHEST, preferred_element_type=F32
        )

    def put_grad(t, position, real, imag):
        value = jnp.concatenate([real, imag], axis=0) * factor
        partial[rounds - 1 - t, :, position] = value.reshape(n, piece, gate)

    def keep(ref, at, pair):
        for i in range(2):
            ref[at, i] = pair[i]

    def kept(ref, at):
        return ref[at, 0], ref[at, 1]

    def one_round(t, carry):
        number = rounds - 1 - t

        def gate_parts(position):
            return split(gates_ref[number, position, 0]), split(gates_ref[number, position, 1])

        real, imag = gate_parts(2)
        last = left_form([reordered(x) for x in real], [reordered(x) for x in imag])
        real, imag = gate_parts(1)
        middle = right_form(real, imag)
        real, imag = gate_parts(0)
        first = left_form(real, imag)

        for which in range(2):
            finish(t, which)
            tick(t, which)

            columns = []
            for a1 in range(blocks):
                pieces = [
                    recv[t, which, a1 * group : (a1 + 1) * group, part, c].reshape(a2, gate)
                    for part in range(2)
                    for c in range(blocks)
                ]
                columns.append(jnp.concatenate(pieces, axis=0))
            values = split(jnp.concatenate(columns, axis=1))
            result = dot3(last, values, ((1,), (0,)))
            for a1 in range(blocks):
                span = slice(a1 * gate, (a1 + 1) * gate)
                rows_buf[span, :gate] = result[:gate, span]
                rows_buf[span, gate:] = result[gate:, span]
            if which == 0:
                keep(wide_before, 0, split(result))
            else:
                outer = dot3(values, kept(wide_before, 0), ((1,), (1,)))
                real, imag = complex_of(outer, gate)
                put_grad(t, 2, restored(real), restored(imag))

            values = split(rows_buf[...])
            result = dot3(values, middle, ((1,), (0,)))
            for a1 in range(blocks):
                for c in range(blocks):
                    low = (a1 * blocks + c) * a2
                    for part in range(2):
                        top = part * gate + a1 * a2
                        cols_buf[top : top + a2, c * gate : (c + 1) * gate] = result[
                            low : low + a2, part * gate : (part + 1) * gate
                        ]
            if which == 0:
                keep(tall_before, 0, split(result))
            else:
                outer = dot3(values, kept(tall_before, 0), ((0,), (0,)))
                put_grad(t, 1, *complex_of(outer, gate))

            values = split(cols_buf[...])
            result = dot3(first, values, ((1,), (0,)))
            for part in range(2):
                for c in range(blocks):
                    block = result[
                        part * gate : (part + 1) * gate, c * gate : (c + 1) * gate
                    ].reshape(n, per, gate)
                    sent[t + 1, which, :, part, c] = block

            @pl.when(t < rounds - 1)
            def _():
                start(t + 1, which)

            if which == 0:
                keep(wide_before, 1, split(result))
            else:
                outer = dot3(values, kept(wide_before, 1), ((1,), (1,)))
                put_grad(t, 0, *complex_of(outer, gate))
        sum_copy(t, None, 0).start()

        return carry

    lax.fori_loop(0, rounds, one_round, 0)

    for which, ref in enumerate((state_out, adjoint_out)):
        for part in range(2):
            for c in range(blocks):
                rows = sent[rounds, which, :, part, c].reshape(gate, gate)
                ref[pl.ds(2 * c + part, gate, stride=stride), :] = rows
    units = [(t, None, 2 * (rounds - 1 - t)) for t in range(rounds)]
    units = [unit for unit in units if unit[2] < stages]
    while units:
        for unit in units:
            advance(*unit)
        units = [(t, position, stage + 1) for t, position, stage in units if stage + 1 < stages]

    def release(t, carry):
        for which in range(2):
            let_go(t, which)
        return carry

    lax.fori_loop(0, rounds, release, 0)


def on_device(state, adjoint, gates):
    gate = gates.shape[-1]
    rounds = gates.shape[0]
    local_size = state.shape[1]
    n = lax.axis_size("qa")
    blocks = local_size // (gate * gate)
    per = gate // n
    factor = 1.0 / math.sqrt(n * local_size // gate)
    steps = n.bit_length() - 1
    piece = 2 * gate // n
    amps = (2, n, 2, blocks, per, gate)
    flat = (2 * local_size // gate, gate)
    sums = (rounds, n, 3, piece, gate)

    def inward(x):
        return x.reshape(2, local_size // gate, gate).swapaxes(0, 1).reshape(flat)

    state_out, adjoint_out, grads = pl.pallas_call(
        functools.partial(kernel, n, rounds, blocks, gate, factor),
        out_shape=(
            jax.ShapeDtypeStruct(flat, F32),
            jax.ShapeDtypeStruct(flat, F32),
            jax.ShapeDtypeStruct(sums, F32),
        ),
        in_specs=[pl.BlockSpec(memory_space=pltpu.VMEM)] * 3,
        out_specs=(pl.BlockSpec(memory_space=pltpu.VMEM),) * 3,
        scratch_shapes=[
            pltpu.VMEM((rounds,) + amps, F32),
            pltpu.VMEM((rounds + 1,) + amps, F32),
            pltpu.VMEM((blocks * gate, 2 * gate), F32),
            pltpu.VMEM((2 * gate, blocks * gate), F32),
            pltpu.VMEM((2, 2, 2 * gate, blocks * gate), BF16),
            pltpu.VMEM((1, 2, blocks * gate, 2 * gate), BF16),
            pltpu.VMEM(sums, F32),
            *[pltpu.VMEM((rounds, n >> (s + 1)) + sums[2:], F32) for s in range(steps)],
            pltpu.SemaphoreType.DMA((rounds, 2, n)),
            pltpu.SemaphoreType.DMA((rounds, 2, n)),
            pltpu.SemaphoreType.DMA((rounds, 2)),
            pltpu.SemaphoreType.DMA((rounds, 2 * steps, 3)),
            pltpu.SemaphoreType.DMA((rounds, 2 * steps, 3)),
        ],
        compiler_params=pltpu.CompilerParams(
            collective_id=0, has_side_effects=True, vmem_limit_bytes=60000 * 1024
        ),
    )(inward(state), inward(adjoint), gates)

    def outward(y):
        return y.reshape(local_size // gate, 2, gate).swapaxes(0, 1).reshape(2, local_size)

    return outward(state_out), outward(adjoint_out), grads.swapaxes(1, 2).reshape(gates.shape)


def solution(mesh):
    amplitudes = P(None, ("grp", "qa"))
    matrices = P("grp", None, None, None, None)
    return jax.shard_map(
        on_device,
        mesh=mesh,
        in_specs=(amplitudes, amplitudes, matrices),
        out_specs=(amplitudes, amplitudes, matrices),
        check_vma=False,
    )
```
